128 devices in a mesh: tm: 4 (over x_hi, core), space: 32 (over x_lo, z, y).
Axes of the slice: x: 4 (x_hi: 2, x_lo: 2; x = x_hi * 2 + x_lo), y: 4, z: 4, core: 2. Of those that a mesh axis runs over, the one named last changes fastest.
Arguments:
- queries: bfloat16 [4, 32, 2, 256, 1536], P('tm', 'space'), may hold values from -8 to 8
- keys: bfloat16 [4, 32, 2, 256, 1536], P('tm', 'space'), may hold values from -6 to 6
- values: bfloat16 [4, 32, 2, 256, 1536], P('tm', 'space'), may hold values from -6 to 6
- tile_mask: int32 [4, 32, 2, 27], P('tm', 'space'), may hold values 0 or 1
- head_reach: int32 [12, 3], replicated, may hold values from 0 to 1, as said below
Outputs:
- attended: bfloat16 [4, 32, 2, 256, 1536], P('tm', 'space')
The draws below stay inside these ranges and needn't reach their ends.
Inputs may be any that keep to these rules, and one draw needn't show every extreme that they name: `head_reach`: some head has reach 1 along all three dimensions.
All inputs are finite; a program needn't handle non-finite values. No bound on the sum of `tile_mask` on one device may be relied on, other than what follows from the above.
Results may differ from the reference program's by a relative error of at most 0.0034.
Values may be sent and summed in bfloat16 or wider, within the bound.
No kernel may reach another device: no remote copies, remote signals or barrier semaphores. Data moves between devices by JAX's collectives and lax.ppermute only.
A program may use at most 320 MiB of HBM per device.

```python
import jax
import jax.numpy as jnp
from jax import lax

HEADS = 12
HD = 128
NWT = 2
TILE = 256
NFT = 4
NHT = 32


def draw_queries(key, part):
    shape = (NFT, NHT, NWT, TILE, HEADS * HD)
    own_key = jax.random.fold_in(key, 1)
    result = jnp.clip(2.0 * jax.random.normal(own_key, shape, jnp.float32), -8.0, 8.0)
    return result.astype(jnp.bfloat16)


def draw_keys(key, part):
    shape = (NFT, NHT, NWT, TILE, HEADS * HD)
    own_key = jax.random.fold_in(key, 2)
    result = jnp.clip(jax.random.normal(own_key, shape, jnp.float32), -6.0, 6.0)
    return result.astype(jnp.bfloat16)


def draw_head_reach(key, part):
    reach = jax.random.randint(jax.random.fold_in(key, 3), (HEADS, 3), 0, 2, dtype=jnp.int32)
    chosen = jax.random.randint(jax.random.fold_in(key, 4), (), 0, HEADS, dtype=jnp.int32)
    full = (jnp.arange(HEADS, dtype=jnp.int32) == chosen).astype(jnp.int32)[:, None]
    return jnp.maximum(reach, full)


def plant(array, key, least, high):
    longest = array.shape.index(max(array.shape))
    spots = []
    for shift in (0, 1):
        where = [jax.random.randint(jax.random.fold_in(key, axis), (), 0, length) for axis, length in enumerate(array.shape)]
        where[longest] = (where[longest] + shift) % array.shape[longest]
        spots.append(tuple(where))
    return array.at[spots[0]].set(least).at[spots[1]].set(high)


def shard_levels(key, shape, shards, low, high):
    gain = 1.0
    for dim, shards_of in shards:
        heights = jax.random.uniform(jax.random.fold_in(jax.random.fold_in(key, 6), dim), (shards_of,), jnp.float32, low / len(shards), high / len(shards))
        gain = gain * jnp.repeat(jnp.exp(heights), shape[dim] // shards_of).reshape((-1,) + (1,) * (len(shape) - 1 - dim))
    return gain


def scatter_about(stream_key, shape, spread, most, shards=(), kind=jnp.bfloat16):
    level = shard_levels(stream_key, shape, shards, -0.22, 0.18) if shards else 1.0
    values = jax.random.normal(stream_key, shape, jnp.float32) * spread * level
    return jnp.minimum(jnp.maximum(values, -most), most).astype(kind)


def setup_inputs(seed: int = 0) -> dict:
    streams_of = jax.random.split(jax.random.key(seed), 6)
    queries = draw_queries(jax.random.fold_in(streams_of[5], 71), 0)
    keys = draw_keys(jax.random.fold_in(streams_of[5], 71), 0)
    values = scatter_about(streams_of[2], (NFT, NHT, NWT, TILE, HEADS * HD), 1.0, 6.0, ((0, 4), (1, 32)))
    tile_mask = plant((jax.random.randint(streams_of[3], (NFT, NHT, NWT, 27), 0, 4) < 3).astype(jnp.int32), jax.random.fold_in(streams_of[3], 1), 0, 1)
    head_reach = draw_head_reach(jax.random.fold_in(streams_of[5], 71), 0)
    return dict(queries=queries, keys=keys, values=values, tile_mask=tile_mask, head_reach=head_reach)


def tile_allow(mask_row, reach, frame_pos, height_pos, width_pos, frame_count, height_count, width_count):
    shift = jnp.arange(3, dtype=jnp.int32) - 1
    frame_step = shift[:, None, None]
    height_step = shift[None, :, None]
    width_step = shift[None, None, :]
    inside = (frame_pos + frame_step >= 0) & (frame_pos + frame_step < frame_count)
    inside = inside & (height_pos + height_step >= 0) & (height_pos + height_step < height_count)
    inside = inside & (width_pos + width_step >= 0) & (width_pos + width_step < width_count)
    picked = mask_row.reshape(3, 3, 3)
    center = (frame_step == 0) & (height_step == 0) & (width_step == 0)
    tile_ok = inside & ((picked == 1) | center)
    within = jnp.abs(frame_step)[None] <= reach[:, 0, None, None, None]
    within = within & (jnp.abs(height_step)[None] <= reach[:, 1, None, None, None])
    within = within & (jnp.abs(width_step)[None] <= reach[:, 2, None, None, None])
    return tile_ok[None] & within


def attend(query_tile, key_rows, value_rows, allow):
    heads = allow.shape[0]
    tile_len = query_tile.shape[0]
    token_allow = jnp.repeat(allow.reshape(heads, -1), tile_len, axis=1)
    highest = lax.Precision.HIGHEST

    def per_head(head):
        query_head = lax.dynamic_slice_in_dim(query_tile, head * HD, HD, 1).astype(jnp.float32)
        key_head = lax.dynamic_slice_in_dim(key_rows, head * HD, HD, 1).astype(jnp.float32)
        value_head = lax.dynamic_slice_in_dim(value_rows, head * HD, HD, 1).astype(jnp.float32)
        usable = token_allow[head]
        scores = jnp.dot(query_head, key_head.T, precision=highest) * (HD ** -0.5)
        scores = jnp.where(usable[None, :], scores, jnp.float32(-1e30))
        largest = jnp.max(scores, axis=1, keepdims=True)
        weights = jnp.where(usable[None, :], jnp.exp(scores - largest), jnp.float32(0.0))
        totals = jnp.sum(weights, axis=1, keepdims=True)
        rounded = weights.astype(jnp.bfloat16).astype(jnp.float32)
        return jnp.dot(rounded, value_head, precision=highest) / totals

    result = lax.map(per_head, jnp.arange(heads, dtype=jnp.int32))
    return jnp.transpose(result, (1, 0, 2)).reshape(tile_len, heads * HD).astype(jnp.bfloat16)


def reference(queries, keys, values, tile_mask, head_reach):
    frame_count, height_count, width_count, tile_len, width = queries.shape
    padding = ((1, 1), (1, 1), (1, 1), (0, 0), (0, 0))
    key_pad = jnp.pad(keys, padding)
    value_pad = jnp.pad(values, padding)
    plane_count = height_count * width_count

    def one_tile(index):
        frame_pos = index // plane_count
        plane_pos = index % plane_count
        height_pos = plane_pos // width_count
        width_pos = plane_pos % width_count
        zero = jnp.int32(0)
        start = (frame_pos, height_pos, width_pos, zero, zero)
        key_rows = lax.dynamic_slice(key_pad, start, (3, 3, 3, tile_len, width)).reshape(-1, width)
        value_rows = lax.dynamic_slice(value_pad, start, (3, 3, 3, tile_len, width)).reshape(-1, width)
        query_tile = lax.dynamic_slice(queries, start, (1, 1, 1, tile_len, width)).reshape(tile_len, width)
        mask_row = lax.dynamic_slice(tile_mask, (frame_pos, height_pos, width_pos, zero), (1, 1, 1, 27)).reshape(27)
        allow = tile_allow(mask_row, head_reach, frame_pos, height_pos, width_pos, frame_count, height_count, width_count)
        return attend(query_tile, key_rows, value_rows, allow)

    result = lax.map(one_tile, jnp.arange(frame_count * plane_count, dtype=jnp.int32))
    return result.reshape(frame_count, height_count, width_count, tile_len, width)
```

```python
import functools
import math

import jax
import jax.numpy as jnp
from jax import lax
from jax.experimental import pallas as pl
from jax.experimental.pallas import tpu as pltpu
from jax.sharding import PartitionSpec as P

HD = 128
SCALE = HD ** (-0.5) * math.log2(math.e)
LOW = -1e30
BF = jnp.bfloat16
F32 = jnp.float32
ANY = pl.BlockSpec(memory_space=pl.ANY)
SMEM = pl.BlockSpec(memory_space=pltpu.SMEM)

BRANCHES = ((12, 12, 12),)

T_HORD, T_FORD, T_HSLOT, T_FSLOT, T_NH, T_NF, T_NC, T_FRAME, T_HEIGHT, T_PICK = (
    0, 16, 32, 48, 64, 65, 66, 67, 68, 69,
)
T_LEN = 80


def shift(value, axis, by):
    count = lax.axis_size(axis)
    return lax.ppermute(value, axis, [(i, i + by) for i in range(count) if 0 <= i + by < count])


def meta_kernel(heads, branches, reach, table):
    def count(member):
        total = jnp.int32(0)
        for h in range(heads):
            total = total + member(h).astype(jnp.int32)
        return total

    def fill(base, slots, groups):
        filled = jnp.int32(0)
        for member in groups:
            for h in range(heads):
                hit = member(h)
                table[jnp.where(hit, base + filled, base + 15)] = jnp.int32(h)
                table[jnp.where(hit, slots + h, slots + 15)] = filled
                filled = filled + hit.astype(jnp.int32)

    frames = lambda h: reach[h, 0] > 0
    heights = lambda h: reach[h, 1] > 0
    corner = lambda h: frames(h) & heights(h)
    fill(T_HORD, T_HSLOT, (corner, lambda h: heights(h) & ~frames(h), lambda h: ~heights(h)))
    fill(T_FORD, T_FSLOT, (corner, lambda h: frames(h) & ~heights(h), lambda h: ~frames(h)))
    nh, nf, nc = count(heights), count(frames), count(corner)
    table[T_NH] = nh
    table[T_NF] = nf
    table[T_NC] = nc
    table[T_FRAME] = lax.axis_index("tm").astype(jnp.int32)
    table[T_HEIGHT] = lax.axis_index("space").astype(jnp.int32)
    pick = jnp.int32(len(branches) - 1)
    for i in reversed(range(len(branches))):
        most_h, most_c, most_f = branches[i]
        fits = (nh <= most_h) & (nc <= most_c) & (nf <= most_f)
        pick = jnp.where(fits, jnp.int32(i), pick)
    table[T_PICK] = pick


def pack_kernel(sizes, table, keys, values, *rest):
    outs, (buf, in_sem, out_sem) = rest[: len(sizes)], rest[len(sizes) :]
    slots = []
    for out, (base, start, size) in zip(outs, sizes):
        slots += [(out, i, base + start + i) for i in range(size)]
    reads = []
    for s, (_, _, where) in enumerate(slots):
        lanes = pl.ds(pl.multiple_of(table[where] * HD, HD), HD)
        pair = [
            pltpu.make_async_copy(a.at[:, :, lanes], buf.at[s, j], in_sem.at[s, j])
            for j, a in enumerate((keys, values))
        ]
        for copy in pair:
            copy.start()
        reads.append(pair)
    writes = []
    for s, (out, i, _) in enumerate(slots):
        for copy in reads[s]:
            copy.wait()
        copy = pltpu.make_async_copy(buf.at[s], out.at[i], out_sem.at[s])
        copy.start()
        writes.append(copy)
    for copy in writes:
        copy.wait()


def scores_of(query, key):
    return lax.dot_general(query, key, (((1,), (1,)), ((), ())), preferred_element_type=F32)


def step(query, tiles, state):
    scores = [scores_of(query, key) for key, _, _ in tiles]
    tops = []
    for s, (_, _, valid) in zip(scores, tiles):
        top = jnp.max(s, axis=1, keepdims=True) * F32(SCALE)
        tops.append(top if valid is None else jnp.where(valid, top, F32(LOW)))
    largest = functools.reduce(jnp.maximum, tops)
    if state is not None:
        old, old_sum, old_acc = state
        largest = jnp.maximum(largest, old)
    total, acc = None, None
    for s, (_, value, valid) in zip(scores, tiles):
        base = largest if valid is None else jnp.where(valid, largest, F32(-LOW))
        weights = jnp.exp2(s * F32(SCALE) - base)
        part = jnp.sum(weights, axis=1, keepdims=True)
        out = jnp.dot(weights.astype(BF), value, preferred_element_type=F32)
        total = part if total is None else total + part
        acc = out if acc is None else acc + out
    if state is not None:
        fade = jnp.exp2(old - largest)
        total = total + fade * old_sum
        acc = acc + fade * old_acc
    return largest, total, acc


def put_stats(ref, where, largest, total):
    lane = lax.broadcasted_iota(jnp.int32, (largest.shape[0], HD), 1)
    ref[where] = jnp.where(lane < HD // 2, largest, total)


def get_stats(stats):
    return stats[:, 0:1], stats[:, HD // 2 : HD // 2 + 1]


def own_kernel(reach, mask, query, key, value, acc_out, stat_out):
    head = pl.program_id(0)
    for c in range(2):
        side = (reach[head, 2] > 0) & (mask[c, 13 + 1 - 2 * c] == 1)
        q = query[c]
        tiles = [(key[c], value[c], None), (key[1 - c], value[1 - c], side)]
        largest, total, acc = step(q, tiles, None)
        acc_out[0, c] = acc
        put_stats(stat_out, (0, c), largest, total)


def far_kernel(spec, last, table, reach, mask, *rest):
    n_bufs = sum(len(s[3]) for s in spec)
    bufs = rest[:n_bufs]
    rest = rest[n_bufs:]
    if last:
        _, query, acc_in, stat_in, out = rest[:5]
        rest = rest[5:]
    else:
        query, acc_in, stat_in, out, acc_out, stat_out = rest[:6]
        rest = rest[6:]
    held, sem, acc_s, max_s, sum_s, lists = rest
    i = pl.program_id(0)
    head = table[T_HORD + i]
    copies = []
    base = 0
    for frame, height, kind, pieces in spec:
        count = table[{"h": T_NH, "f": T_NF, "c": T_NC}[kind]]
        size = 0
        for ref, start, length in pieces:
            for j in range(length):
                slot = base + start + j
                copies.append(
                    (pltpu.make_async_copy(bufs[ref].at[j], held.at[slot], sem.at[slot]), start + j < count)
                )
            size += length
        base += size

    @pl.when(i == 0)
    def _():
        for copy, wanted in copies:
            pl.when(wanted)(copy.start)

    counts = [jnp.int32(0), jnp.int32(0)]
    base = 0
    for frame, height, kind, pieces in spec:
        size = sum(p[2] for p in pieces)
        slot = table[(T_FSLOT if kind == "f" else T_HSLOT) + head]
        at_frame = table[T_FRAME] + frame
        at_height = table[T_HEIGHT] + height
        reaches = True
        if frame:
            reaches = reaches & (reach[head, 0] > 0)
        if height:
            reaches = reaches & (reach[head, 1] > 0)
        here = base + jnp.where(reaches, slot, 0)

        @pl.when(reaches)
        def _(here=here):
            pltpu.make_async_copy(bufs[0].at[0], held.at[here], sem.at[here]).wait()

        inside = (at_frame >= 0) & (at_frame < lax.axis_size("tm"))
        inside = inside & (at_height >= 0) & (at_height < lax.axis_size("space")) & reaches
        for c in range(2):
            for w in range(2):
                g = w - c
                ok = inside & (mask[c, 9 * (frame + 1) + 3 * (height + 1) + g + 1] == 1)
                if g:
                    ok = ok & (reach[head, 2] > 0)
                lists[c, counts[c]] = here * 2 + w
                counts[c] = counts[c] + ok.astype(jnp.int32)
        base += size

    state = []
    for c in range(2):
        largest, total = get_stats(stat_in[0, c])
        acc_s[c] = acc_in[0, c]
        max_s[c] = jnp.broadcast_to(largest, (largest.shape[0], HD))
        sum_s[c] = jnp.broadcast_to(total, (total.shape[0], HD))

    spare = jnp.where(counts[0] > 0, lists[0, 0], lists[1, 0])

    def body(it, carry):
        for c in range(2):
            tiles = []
            for t in range(2):
                place = 2 * it + t
                valid = place < counts[c]
                entry = jnp.where(valid, lists[c, place], spare)
                slot, w = entry // 2, entry % 2
                tiles.append((held[slot, 0, w], held[slot, 1, w], valid))
            q = query[c]
            largest, total, acc = step(q, tiles, (max_s[c][:, 0:1], sum_s[c][:, 0:1], acc_s[c]))
            acc_s[c] = acc
            max_s[c] = jnp.broadcast_to(largest, (largest.shape[0], HD))
            sum_s[c] = jnp.broadcast_to(total, (total.shape[0], HD))
        return carry

    rounds = (jnp.maximum(counts[0], counts[1]) + 1) // 2
    lax.fori_loop(0, rounds, body, 0)
    for c in range(2):
        out[c] = (acc_s[c] / sum_s[c][:, 0:1]).astype(BF)
        if not last:
            acc_out[0, c] = acc_s[c]
            put_stats(stat_out, (0, c), max_s[c][:, 0:1], sum_s[c][:, 0:1])


def branch(most_h, most_c, most_f, queries, keys, values, mask, reach, table):
    nw, tile, width = queries.shape
    heads = width // HD
    unit = (2, nw, tile, HD)
    rest_h = most_h - most_c
    sizes = [(T_HORD, 0, most_c)]
    if rest_h:
        sizes.append((T_HORD, most_c, rest_h))
    sizes.append((T_FORD, 0, most_f))
    slots = most_h + most_f
    packed = pl.pallas_call(
        functools.partial(pack_kernel, sizes),
        name="pack",
        in_specs=[SMEM, ANY, ANY],
        out_specs=[ANY] * len(sizes),
        out_shape=[jax.ShapeDtypeStruct((n,) + unit, BF) for _, _, n in sizes],
        scratch_shapes=[
            pltpu.VMEM((slots,) + unit, BF),
            pltpu.SemaphoreType.DMA((slots, 2)),
            pltpu.SemaphoreType.DMA((slots,)),
        ],
        cost_estimate=pl.CostEstimate(flops=0, bytes_accessed=slots << 19, transcendentals=0),
    )(table, keys, values)
    first = packed[0]
    low1, high1 = shift(first, "space", 1), shift(first, "space", -1)
    frame_lo, frame_hi = shift(packed[-1], "tm", 1), shift(packed[-1], "tm", -1)
    corners = [shift(b, "tm", by) for by in (1, -1) for b in (low1, high1)]
    if rest_h:
        low2, high2 = shift(packed[1], "space", 1), shift(packed[1], "space", -1)

    block = pl.BlockSpec((nw, tile, HD), lambda i: (0, 0, i))
    state_block = pl.BlockSpec((1, nw, tile, HD), lambda i: (i, 0, 0, 0))
    state = jax.ShapeDtypeStruct((heads, nw, tile, HD), F32)
    acc, stats = pl.pallas_call(
        own_kernel,
        name="own",
        grid=(heads,),
        in_specs=[SMEM, SMEM, block, block, block],
        out_specs=[state_block, state_block],
        out_shape=[state, state],
        cost_estimate=pl.CostEstimate(
            flops=heads * 4 * 4 * tile * tile * HD, bytes_accessed=12 << 20, transcendentals=heads * 4 * tile * tile
        ),
    )(reach, mask, queries, keys, values)

    def far(spec, bufs, last, steps, slots, previous, acc, stats):
        order = lambda i, table, reach, mask: (0, 0, table[T_HORD + i])
        by_head = lambda i, table, reach, mask: (table[T_HORD + i], 0, 0, 0)
        by_slot = lambda i, table, reach, mask: (i, 0, 0, 0)
        data = pl.BlockSpec((nw, tile, HD), order)
        head_state = pl.BlockSpec((1, nw, tile, HD), by_slot if last else by_head)
        slot_state = pl.BlockSpec((1, nw, tile, HD), by_slot)
        in_specs = [ANY] * len(bufs) + ([ANY] if last else []) + [data, head_state, head_state]
        out_specs = [data] if last else [data, slot_state, slot_state]
        out_shape = [jax.ShapeDtypeStruct((nw, tile, width), BF)]
        if not last:
            out_shape += [state, state]
        args = list(bufs) + ([previous] if last else []) + [queries, acc, stats]
        entries = sum(len(s[3]) for s in spec)
        return pl.pallas_call(
            functools.partial(far_kernel, spec, last),
            name="corner" if last else "near",
            grid_spec=pltpu.PrefetchScalarGridSpec(
                num_scalar_prefetch=3,
                grid=(steps,),
                in_specs=in_specs,
                out_specs=out_specs,
                scratch_shapes=[
                    pltpu.VMEM((slots,) + unit, BF),
                    pltpu.SemaphoreType.DMA((slots,)),
                    pltpu.VMEM((nw, tile, HD), F32),
                    pltpu.VMEM((nw, tile, HD), F32),
                    pltpu.VMEM((nw, tile, HD), F32),
                    pltpu.SMEM((nw, 16), jnp.int32),
                ],
            ),
            out_shape=out_shape,
            input_output_aliases={3 + len(bufs): 0} if last else {},
            cost_estimate=pl.CostEstimate(
                flops=slots * 4 * tile * tile * HD * 4, bytes_accessed=slots << 18, transcendentals=slots * 4 * tile * tile
            ),
        )(table, reach, mask, *args)

    bufs, spec = [], []
    for height, parts in ((-1, [low1] + ([low2] if rest_h else [])), (1, [high1] + ([high2] if rest_h else []))):
        pieces, start = [], 0
        for part in parts:
            pieces.append((len(bufs), start, part.shape[0]))
            start += part.shape[0]
            bufs.append(part)
        spec.append((0, height, "h", pieces))
    for frame, part in ((-1, frame_lo), (1, frame_hi)):
        spec.append((frame, 0, "f", [(len(bufs), 0, most_f)]))
        bufs.append(part)
    out, acc, stats = far(spec, bufs, False, heads, 2 * (most_h + most_f), None, acc, stats)
    spec = [(f, e, "c", [(j, 0, most_c)]) for j, (f, e) in enumerate(((-1, -1), (-1, 1), (1, -1), (1, 1)))]
    (out,) = far(spec, corners, True, most_c, 4 * most_c, out, acc, stats)
    return out


def local(queries, keys, values, tile_mask, head_reach):
    queries, keys, values, mask = queries[0, 0], keys[0, 0], values[0, 0], tile_mask[0, 0]
    heads = queries.shape[2] // HD
    table = pl.pallas_call(
        functools.partial(meta_kernel, heads, BRANCHES),
        name="meta",
        in_specs=[SMEM],
        out_specs=SMEM,
        out_shape=jax.ShapeDtypeStruct((T_LEN,), jnp.int32),
    )(head_reach)
    run = [functools.partial(branch, *sizes) for sizes in BRANCHES]
    args = (queries, keys, values, mask, head_reach, table)
    if len(run) == 1:
        out = run[0](*args)
    else:
        out = lax.switch(table[T_PICK], run, *args)
    return out[None, None]


def solution(mesh):
    in_specs = (
        P("tm", "space", None, None, None),
        P("tm", "space", None, None, None),
        P("tm", "space", None, None, None),
        P("tm", "space", None, None),
        P(),
    )
    out_specs = P("tm", "space", None, None, None)
    return jax.shard_map(local, mesh=mesh, in_specs=in_specs, out_specs=out_specs, check_vma=False)
```
